256 devices in a mesh: section: 8 (over y, core), expert: 32 (over x, z).
Axes of the slice: x: 4, y: 4, z: 8, core: 2. Of those that a mesh axis runs over, the one named last changes fastest.
Arguments:
- handoff: bfloat16 [8, 4096, 2048], P('section', 'expert'), may hold values from -6 to 6
- cotangent_handoff: bfloat16 [8, 4096, 2048], P('section', 'expert'), may hold values from -6 to 6
- saved_input: bfloat16 [8, 4096, 2048], P('section', 'expert'), may hold values from -6 to 6
- norm_gain: float32 [8, 2048], P('section'), may hold values from 0.1 to 1.9
- w_gate: bfloat16 [8, 32, 2048, 768], P('section', 'expert'), may hold values from -0.125 to 0.125
- w_up: bfloat16 [8, 32, 2048, 768], P('section', 'expert'), may hold values from -0.125 to 0.125
- w_down: bfloat16 [8, 32, 768, 2048], P('section', 'expert'), may hold values from -1.25 to 1.25
- picks_fwd: int32 [8, 4096, 8], P('section', 'expert'), may hold values from 0 to 127, as said below
- picks_bwd: int32 [8, 4096, 8], P('section', 'expert'), may hold values from 0 to 127, as said below
- gates_fwd: float32 [8, 4096, 8], P('section', 'expert'), may hold values from 0.05 to 1
- gates_bwd: float32 [8, 4096, 8], P('section', 'expert'), may hold values from 0.05 to 1
Outputs:
- act_out: bfloat16 [8, 4096, 2048], P('section', 'expert')
- grad_out: bfloat16 [8, 4096, 2048], P('section', 'expert')
The draws below stay inside these ranges and needn't reach their ends.
Inputs may be any that keep to these rules, and one draw needn't show every extreme that they name: `picks_fwd`: each row names 8 different experts. Among the 128 tokens of one section that one expert device holds, no expert is named more than 16 times, and one expert with id below 32 is named exactly 16 times among the tokens of every such device. `picks_bwd`: each row names 8 different experts. Among the 128 tokens of one section that one expert device holds, no expert is named more than 16 times, and one expert with id below 32 is named exactly 16 times among the tokens of every such device.
All inputs are finite; a program needn't handle non-finite values.
Results may differ from the reference program's by a relative error of at most 0.0064.
Values may be sent and summed in bfloat16 or wider, within the bound.
A program may use at most 128 MiB of HBM per device.

```python
import math
import jax
import jax.numpy as jnp
from jax import lax

D = 2048
HID = 768
NUM_ALL = 128
TOP = 8
TOK_DEV = 128
SECTIONS = 8
EXPERTS = 32
TOKENS = 4096
CAP = 16


def route_draw(key):
    group = NUM_ALL // TOP
    k_perm, k_hot, k_rows, k_vals = jax.random.split(key, 4)
    perm = jax.random.permutation(k_perm, NUM_ALL).astype(jnp.int32)
    hot = jax.random.randint(k_hot, (), 0, EXPERTS).astype(jnp.int32)
    labels = jnp.where(perm == hot, perm[0], perm).at[0].set(hot).reshape(TOP, group)
    level = jnp.arange(1, group, dtype=jnp.int32)
    lower = CAP + (TOK_DEV - CAP) * ((level - 1) * (level + group - 2)) // ((group - 1) * (2 * group - 2))
    classes = jnp.sum((jnp.arange(TOK_DEV, dtype=jnp.int32)[:, None] >= lower[None, :]).astype(jnp.int32), axis=1)
    count = SECTIONS * EXPERTS * TOP
    row_keys = jax.random.split(k_rows, count)
    val_keys = jax.random.split(k_vals, count)
    row_order = jax.vmap(lambda k: jax.random.permutation(k, TOK_DEV))(row_keys).astype(jnp.int32)
    value_order = jax.vmap(lambda k: jax.random.permutation(k, group))(val_keys).astype(jnp.int32)
    slot_index = jnp.arange(count, dtype=jnp.int32) % TOP
    fixed = jnp.where(value_order == 0, value_order[:, :1], value_order)
    fixed = fixed.at[:, 0].set(0)
    value_order = jnp.where((slot_index == 0)[:, None], fixed, value_order)
    row_class = classes[row_order]
    chosen = jnp.take_along_axis(value_order, row_class, axis=1)
    picks = labels[slot_index[:, None], chosen]
    picks = picks.reshape(SECTIONS, EXPERTS, TOP, TOK_DEV).transpose(0, 1, 3, 2).reshape(SECTIONS, TOKENS, TOP)
    return picks.astype(jnp.int32)


def draw_picks_fwd(key, part):
    return route_draw(jax.random.fold_in(key, 11))


def draw_picks_bwd(key, part):
    return route_draw(jax.random.fold_in(key, 23))


def block_scale(key, extent, pieces, smallest, high):
    factor_of, own = 1.0, jax.random.fold_in(key, 6)
    for dim, parts in pieces:
        draws = jnp.exp(jax.random.uniform(jax.random.fold_in(own, dim), (parts,), jnp.float32, smallest / len(pieces), high / len(pieces)))
        factor_of = factor_of * jnp.repeat(draws, extent[dim] // parts).reshape([-1 if axis == dim else 1 for axis in range(len(extent))])
    return factor_of


def bell_draw(key, extent, width, bound, pieces=(), kind=jnp.bfloat16):
    factor_of = block_scale(key, extent, pieces, -0.22, 0.18) if pieces else 1.0
    drawn = jax.random.normal(key, extent, jnp.float32) * width * factor_of
    return jnp.minimum(jnp.maximum(drawn, -bound), bound).astype(kind)


def setup_inputs(seed: int = 0) -> dict:
    arg_keys = jax.random.split(jax.random.key(seed), 12)
    handoff = bell_draw(arg_keys[0], (SECTIONS, TOKENS, D), 1.0, 6.0, ((0, 8), (1, 32)))
    cotangent_handoff = bell_draw(arg_keys[1], (SECTIONS, TOKENS, D), 1.0, 6.0, ((0, 8), (1, 32)))
    saved_input = bell_draw(arg_keys[2], (SECTIONS, TOKENS, D), 1.0, 6.0, ((0, 8), (1, 32)))
    norm_gain = jnp.clip(1.0 + 0.18 * jax.random.normal(arg_keys[3], (SECTIONS, D), jnp.float32), 0.1, 1.9)
    w_gate = bell_draw(arg_keys[4], (SECTIONS, EXPERTS, D, HID), D ** -0.5, 0.125, ((0, 8), (1, 32)))
    w_up = bell_draw(arg_keys[5], (SECTIONS, EXPERTS, D, HID), D ** -0.5, 0.125, ((0, 8), (1, 32)))
    w_down = bell_draw(arg_keys[6], (SECTIONS, EXPERTS, HID, D), (HID // 32) ** -0.5, 1.25, ((0, 8), (1, 32)))
    picks_fwd = draw_picks_fwd(jax.random.fold_in(arg_keys[11], 71), 0)
    picks_bwd = draw_picks_bwd(jax.random.fold_in(arg_keys[11], 71), 0)
    gates_fwd = jnp.clip(jnp.exp(math.log(1.0) - 2.9957323 * jax.random.uniform(arg_keys[9], (SECTIONS, TOKENS, TOP), jnp.float32) ** block_scale(arg_keys[9], (SECTIONS, TOKENS, TOP), ((0, 8), (1, 32)), -0.2, 0.2)), 0.05, 1.0)
    gates_bwd = jnp.clip(jnp.exp(math.log(1.0) - 2.9957323 * jax.random.uniform(arg_keys[10], (SECTIONS, TOKENS, TOP), jnp.float32) ** block_scale(arg_keys[10], (SECTIONS, TOKENS, TOP), ((0, 8), (1, 32)), -0.2, 0.2)), 0.05, 1.0)
    return {"handoff": handoff, "cotangent_handoff": cotangent_handoff, "saved_input": saved_input, "norm_gain": norm_gain, "w_gate": w_gate, "w_up": w_up, "w_down": w_down, "picks_fwd": picks_fwd, "picks_bwd": picks_bwd, "gates_fwd": gates_fwd, "gates_bwd": gates_bwd}


EPS = 1e-06

def normalize(rows, gain):
    values = rows.astype(jnp.float32)
    scale = lax.rsqrt(lax.optimization_barrier(jnp.mean(values * values, axis=-1)) + EPS)
    return ((values * scale[:, None] * gain[None, :]).astype(jnp.bfloat16), scale)

def transposed(left, right):
    return lax.dot_general(left, right, (((1,), (1,)), ((), ())), preferred_element_type=jnp.float32)

def expert_forward(rows, w_g, w_u, w_d):
    gate_act = jnp.dot(rows, w_g, preferred_element_type=jnp.float32)
    up_act = jnp.dot(rows, w_u, preferred_element_type=jnp.float32)
    hidden = (jax.nn.silu(gate_act) * up_act).astype(jnp.bfloat16)
    return jnp.dot(hidden, w_d, preferred_element_type=jnp.float32).astype(jnp.bfloat16)

def expert_backward(rows, scaled_cot, w_g, w_u, w_d):
    gate_act = jnp.dot(rows, w_g, preferred_element_type=jnp.float32)
    up_act = jnp.dot(rows, w_u, preferred_element_type=jnp.float32)
    sigma = jax.nn.sigmoid(gate_act)
    hid_grad = transposed(scaled_cot, w_d)
    gate_grad = (hid_grad * up_act * sigma * (1.0 + gate_act * (1.0 - sigma))).astype(jnp.bfloat16)
    up_grad = (hid_grad * gate_act * sigma).astype(jnp.bfloat16)
    return (transposed(gate_grad, w_g) + transposed(up_grad, w_u)).astype(jnp.bfloat16)

def section_pass(arriving, upstream, saved, gain, w_g, w_u, w_d, pick_f, pick_b, gate_f, gate_b):
    slots = CAP * EXPERTS
    fwd_normed, unused_scale = normalize(arriving, gain)
    bwd_normed, bwd_scale = normalize(saved, gain)
    fwd_weight = gate_f / lax.optimization_barrier(jnp.sum(gate_f, axis=1, keepdims=True))
    bwd_weight = gate_b / lax.optimization_barrier(jnp.sum(gate_b, axis=1, keepdims=True))
    order = jnp.arange(TOKENS, dtype=jnp.int32)

    def rows_of(picks, weight, expert):
        named = picks == expert
        has = jnp.any(named, axis=1)
        share = lax.optimization_barrier(jnp.sum(jnp.where(named, weight, jnp.float32(0.0)), axis=1))
        place = (jnp.cumsum(has.astype(jnp.int32)) - 1).astype(jnp.int32)
        place = jnp.where(has, place, slots).astype(jnp.int32)
        index = jnp.zeros((slots,), jnp.int32).at[place].set(order, mode='drop')
        live = jnp.zeros((slots,), jnp.float32).at[place].set(jnp.float32(1.0), mode='drop')
        return (index, live, share[index])

    def visit(carry, expert):
        fwd_acc, bwd_acc = carry
        index, live, share = rows_of(pick_f, fwd_weight, expert)
        out_rows = expert_forward(fwd_normed[index], w_g[expert], w_u[expert], w_d[expert])
        fwd_acc = fwd_acc.at[index].add((live * share)[:, None] * out_rows.astype(jnp.float32))
        index_b, live_b, share_b = rows_of(pick_b, bwd_weight, expert)
        scaled_cot = (share_b[:, None] * upstream[index_b].astype(jnp.float32)).astype(jnp.bfloat16)
        grads = expert_backward(bwd_normed[index_b], scaled_cot, w_g[expert], w_u[expert], w_d[expert])
        bwd_acc = bwd_acc.at[index_b].add(live_b[:, None] * grads.astype(jnp.float32))
        return ((fwd_acc, bwd_acc), None)
    start = (jnp.zeros((TOKENS, D), jnp.float32), jnp.zeros((TOKENS, D), jnp.float32))
    (fwd_acc, normed_grad), unused = lax.scan(visit, start, jnp.arange(EXPERTS, dtype=jnp.int32))
    act = (arriving.astype(jnp.float32) + fwd_acc).astype(jnp.bfloat16)
    values = saved.astype(jnp.float32)
    gained = gain[None, :] * normed_grad
    cube = bwd_scale * bwd_scale * bwd_scale
    grad = (upstream.astype(jnp.float32) + bwd_scale[:, None] * gained - values * cube[:, None] * lax.optimization_barrier(jnp.mean(values * gained, axis=1, keepdims=True))).astype(jnp.bfloat16)
    return (act, grad)

def reference(handoff, cotangent_handoff, saved_input, norm_gain, w_gate, w_up, w_down, picks_fwd, picks_bwd, gates_fwd, gates_bwd):
    acts = []
    grads = []
    for section in range(SECTIONS):
        act, grad = section_pass(handoff[(section - 1) % SECTIONS], cotangent_handoff[(section + 1) % SECTIONS], saved_input[section], norm_gain[section], w_gate[section], w_up[section], w_down[section], picks_fwd[section], picks_bwd[section], gates_fwd[section], gates_bwd[section])
        acts.append(act)
        grads.append(grad)
    return (jnp.stack(acts), jnp.stack(grads))
```

```python
import functools

import jax
import jax.numpy as jnp
from jax import lax
from jax.experimental import pallas as pl
from jax.experimental.pallas import tpu as pltpu
from jax.sharding import PartitionSpec as P

EPS = 1e-06
MESH = pl.DeviceIdType.MESH
F32 = jnp.float32
BF16 = jnp.bfloat16

NX = 4
NZ = 8
SEC = 8
CAP = 16
TOK = 128
D = 2048
HID = 768
CLS = 4 * CAP
FULL = (128, 128, 128, 64)
ORDER = (0, 1, 7, 2, 6, 3, 5, 4)


def where_am_i():
    e = lax.axis_index("expert")
    return lax.axis_index("section"), e // NZ, e % NZ


def at(s, x, z):
    return (s, x * NZ + z)


def iota(shape, dim):
    return lax.broadcasted_iota(jnp.int32, shape, dim)


def one(cond):
    return jnp.where(cond, jnp.float32(1.0), jnp.float32(0.0))


def routing(picks, gates, x, z):
    tok = iota((TOK, TOK), 1)
    sub = iota((TOK, TOK), 0)
    weight = gates / jnp.sum(gates, axis=0, keepdims=True)
    lane_e = iota((32, TOK), 0)
    disp = lane_e // 4
    expert = ((x + lane_e % 4) % NX) * NZ + (z + disp) % NZ
    named = jnp.zeros((32, TOK), F32)
    share = jnp.zeros((32, TOK), F32)
    for j in range(picks.shape[0]):
        hit = picks[j : j + 1, :] == expert
        named = named + one(hit)
        share = share + jnp.where(hit, weight[j : j + 1, :], 0.0)
    place = jnp.dot(
        named.astype(BF16), one(sub < tok).astype(BF16), preferred_element_type=F32
    )
    dist = disp.astype(F32)
    up = jnp.max(named * jnp.where(disp < 4, dist, 0.0), axis=0, keepdims=True)
    down = jnp.max(named * jnp.where(disp > 4, 8.0 - dist, 0.0), axis=0, keepdims=True)
    far = jnp.max(jnp.where(disp == 4, named, 0.0), axis=0, keepdims=True)
    even = one(iota((1, TOK), 1) % 2 == 0)
    go_up = jnp.where(up == down, even, one(up > down))
    up = jnp.where(far * go_up > 0.0, 4.0, up)
    down = jnp.where(far * (1.0 - go_up) > 0.0, 4.0, down)

    def ranks(reach):
        row = jnp.broadcast_to(reach, (TOK, TOK))
        col = jnp.sum(jnp.where(sub == tok, row, 0.0), axis=1, keepdims=True)
        col = jnp.broadcast_to(col, (TOK, TOK))
        ahead = jnp.where(row > col, 1.0, jnp.where(row == col, one(tok < sub), 0.0))
        pos_col = jnp.sum(ahead, axis=1, keepdims=True)
        ahead = jnp.where(col > row, 1.0, jnp.where(row == col, one(sub < tok), 0.0))
        pos_row = jnp.sum(ahead, axis=0, keepdims=True)
        return pos_row, pos_col

    up_row, up_col = ranks(up)
    down_row, down_col = ranks(down)
    own = iota((1, TOK), 1).astype(F32)
    split = jnp.where(go_up > 0.0, up_row, down_row + 128.0)
    value = jnp.where(
        disp == 0, own, jnp.where(disp < 4, up_row, jnp.where(disp == 4, split, down_row))
    )
    slot = iota((32, CAP, TOK), 1).astype(F32)
    chosen = jnp.where(place[:, None, :] == slot, named[:, None, :], 0.0)
    index = jnp.sum(chosen * (value + 1.0)[:, None, :], axis=2, keepdims=True) - 1.0
    scale = jnp.sum(chosen * share[:, None, :], axis=2, keepdims=True)
    index = index.reshape(32 * CAP, 1)
    scale = scale.reshape(32 * CAP, 1)
    return index, scale, (up_row, down_row), (up_col, down_col), (up, down)


def prepare_kernel(
    caps,
    handoff,
    cotangent,
    picks_f,
    gates_f,
    picks_b,
    gates_b,
    arriving,
    upstream,
    meta,
    meta_t,
    pos,
    pos_t,
    flag,
    meta_send,
    flag_x,
    flag_s,
    big_send,
    big_recv,
    meta_ss,
    meta_rs,
    x_ss,
    x_rs,
    s_ss,
    s_rs,
):
    s, x, z = where_am_i()
    z_peer = lambda d: at(s, x, (z + d) % NZ)
    x_peer = lambda d: at(s, (x + d) % NX, z)
    s_peer = lambda d: at((s + d) % SEC, x, z)
    barrier = pltpu.get_barrier_semaphore()
    partners = (
        [z_peer(d) for d in range(1, NZ)]
        + [x_peer(d) for d in range(1, NX)]
        + [s_peer(d) for d in range(1, SEC)]
    )
    for peer in partners:
        pl.semaphore_signal(barrier, inc=1, device_id=peer, device_id_type=MESH)
    pl.semaphore_wait(barrier, len(partners))
    big = [
        pltpu.make_async_remote_copy(
            src, dst, big_send.at[i], big_recv.at[i], device_id=peer, device_id_type=MESH
        )
        for i, (src, dst, peer) in enumerate(
            ((handoff, arriving, s_peer(1)), (cotangent, upstream, s_peer(SEC - 1)))
        )
    ]
    for copy in big:
        copy.start()

    lane = iota((CLS, TOK), 1)
    table = jnp.zeros((CLS, TOK), F32)
    over = jnp.zeros((1, 1), F32)
    lane_t = iota((TOK, TOK), 1)
    columns = jnp.zeros((TOK, TOK), F32)
    for m, (picks, gates) in enumerate(((picks_f, gates_f), (picks_b, gates_b))):
        index, scale, rows, cols, reach = routing(picks[...], gates[...], x, z)
        for d in range(NZ):
            part = slice(d * CLS, (d + 1) * CLS)
            table = jnp.where(lane == 8 * d + 2 * m, index[part], table)
            table = jnp.where(lane == 8 * d + 2 * m + 1, scale[part], table)
        for i in range(2):
            pos[2 * m + i : 2 * m + i + 1, :] = rows[i]
            columns = jnp.where(lane_t == 2 * m + i, cols[i], columns)
            for k in range(4):
                count = jnp.sum(one(reach[i] > k + 0.5), axis=1, keepdims=True)
                over = jnp.maximum(over, one(count > caps[k] + 0.5))
    pos[4:8, :] = jnp.zeros((4, TOK), F32)
    pos_t[...] = columns
    whole = jnp.concatenate([table, jnp.zeros((CLS, TOK), F32)], axis=0)
    whole = jnp.transpose(whole)[:CLS, :]
    whole = jnp.where(iota((CLS, TOK), 0) % 8 == 4, jnp.broadcast_to(over, (CLS, TOK)), whole)
    meta_send[...] = whole
    meta[0:8, :] = whole[0:8, :]
    copies = []
    for d in range(1, NZ):
        part = pl.ds(8 * d, 8)
        copy = pltpu.make_async_remote_copy(
            meta_send.at[part],
            meta.at[part],
            meta_ss.at[d],
            meta_rs.at[d],
            device_id=z_peer(d),
            device_id_type=MESH,
        )
        copy.start()
        copies.append(copy)
    for copy in copies:
        copy.wait()
    got = meta[...]
    meta_t[...] = jnp.transpose(jnp.concatenate([got, jnp.zeros((CLS, TOK), F32)], axis=0))
    over = jnp.max(
        jnp.where(iota((CLS, TOK), 0) % 8 == 4, got, 0.0), axis=0, keepdims=True
    )

    def spread(over, buf, peers, send, recv):
        buf[0] = jnp.broadcast_to(over, (8, TOK))
        copies = []
        for d, peer in enumerate(peers, 1):
            copy = pltpu.make_async_remote_copy(
                buf.at[0],
                buf.at[d],
                send.at[d],
                recv.at[d],
                device_id=peer,
                device_id_type=MESH,
            )
            copy.start()
            copies.append(copy)
        for copy in copies:
            copy.wait()
        return jnp.max(jnp.max(buf[...], axis=0), axis=0, keepdims=True)

    over = spread(over, flag_x, [x_peer(d) for d in range(1, NX)], x_ss, x_rs)
    over = spread(over, flag_s, [s_peer(d) for d in range(1, SEC)], s_ss, s_rs)
    flag[...] = jnp.broadcast_to(over, (8, TOK))
    for copy in big:
        copy.wait()


def prepare(caps, handoff, cotangent, picks_f, gates_f, picks_b, gates_b):
    vmem = pl.BlockSpec(memory_space=pltpu.VMEM)
    hbm = pl.BlockSpec(memory_space=pl.ANY)
    rows = jax.ShapeDtypeStruct((TOK, D), BF16)
    sem = pltpu.SemaphoreType.DMA
    return pl.pallas_call(
        functools.partial(prepare_kernel, caps),
        out_shape=(
            rows,
            rows,
            jax.ShapeDtypeStruct((CLS, TOK), F32),
            jax.ShapeDtypeStruct((TOK, TOK), F32),
            jax.ShapeDtypeStruct((8, TOK), F32),
            jax.ShapeDtypeStruct((TOK, TOK), F32),
            jax.ShapeDtypeStruct((8, TOK), F32),
        ),
        in_specs=[hbm, hbm, vmem, vmem, vmem, vmem],
        out_specs=(hbm, hbm, vmem, vmem, vmem, vmem, vmem),
        scratch_shapes=[
            pltpu.VMEM((CLS, TOK), F32),
            pltpu.VMEM((NX, 8, TOK), F32),
            pltpu.VMEM((SEC, 8, TOK), F32),
            sem((2,)),
            sem((2,)),
            sem((NZ,)),
            sem((NZ,)),
            sem((NX,)),
            sem((NX,)),
            sem((SEC,)),
            sem((SEC,)),
        ],
        name="prepare",
        compiler_params=pltpu.CompilerParams(collective_id=0, has_side_effects=True),
    )(handoff, cotangent, picks_f, gates_f, picks_b, gates_b)


R_, C_, F_ = 0, 1, 2
G_, O_ = 0, 1


def layer_kernel(
    caps,
    saved,
    arriving,
    upstream,
    gain,
    meta,
    meta_t,
    pos,
    pos_t,
    w_gate,
    w_up,
    w_down,
    act,
    grad,
    wg,
    wu,
    wd,
    first,
    zbuf,
    xs,
    xr,
    yr,
    sb,
    rb,
    hid,
    scale_ref,
    w_sem,
    z_ss,
    z_rs,
    x_ss,
    x_rs,
    y_ss,
    y_rs,
    r_ss,
    r_rs,
):
    s, x, z = where_am_i()
    z_peer = lambda d: at(s, x, (z + d + NZ) % NZ)
    x_peer = lambda d: at(s, (x + d + NX) % NX, z)
    offs = [sum(caps[:k]) for k in range(5)]
    weights = [
        pltpu.make_async_copy(src, dst, w_sem.at[i])
        for i, (src, dst) in enumerate(((w_gate, wg), (w_up, wu), (w_down, wd)))
    ]
    for copy in weights:
        copy.start()
    barrier = pltpu.get_barrier_semaphore()
    partners = [z_peer(1), z_peer(-1), x_peer(1), x_peer(2), x_peer(3)]
    for peer in partners:
        pl.semaphore_signal(barrier, inc=1, device_id=peer, device_id_type=MESH)
    pl.semaphore_wait(barrier, len(partners))

    sends = []

    def remote(src, dst, send, recv, peer):
        copy = pltpu.make_async_remote_copy(
            src, dst, send, recv, device_id=peer, device_id_type=MESH
        )
        copy.start()
        sends.append(copy)
        return copy

    def normalize(ref):
        values = ref[...].astype(F32)
        scale = lax.rsqrt(jnp.mean(values * values, axis=-1, keepdims=True) + EPS)
        return (values * scale * gain[...]).astype(BF16), scale

    hops = {}

    def hop(stream, k):
        for way in range(2):
            part = pl.ds(offs[k - 1], caps[k - 1])
            if k == 1:
                src = first.at[stream, way, pl.ds(0, caps[0])]
            else:
                src = zbuf.at[stream, way, pl.ds(offs[k - 2], caps[k - 1])]
            hops[stream, way, k] = remote(
                src,
                zbuf.at[stream, way, part],
                z_ss.at[stream, way, k - 1],
                z_rs.at[stream, way, k - 1],
                z_peer(1 - 2 * way),
            )

    def sort_rows(stream, rows):
        m = 0 if stream == F_ else 1
        for way in range(2):
            order = pos[2 * m + way : 2 * m + way + 1, :]
            perm = one(order == iota((TOK, TOK), 0).astype(F32)).astype(BF16)
            first[stream, way] = jnp.dot(perm, rows, preferred_element_type=F32).astype(BF16)

    xcopies = {}

    def gather(stream, d, rows):
        m = 0 if stream == F_ else 1
        index = meta_t[0:CLS, 8 * d + 2 * m : 8 * d + 2 * m + 1]
        total = None
        for values, base in rows:
            n = values.shape[0]
            sel = one(index == (iota((CLS, n), 1) + base).astype(F32)).astype(BF16)
            part = jnp.dot(sel, values, preferred_element_type=F32)
            total = part if total is None else total + part
        if stream == C_:
            total = total * meta_t[0:CLS, 8 * d + 3 : 8 * d + 4]
        total = total.astype(BF16)
        base = ORDER.index(d) * CLS
        xr[stream, base : base + CAP, :] = total[0:CAP]
        xs[stream, base + CAP : base + CLS, :] = total[CAP:CLS]
        for o in range(1, NX):
            part = pl.ds(base + o * CAP, CAP)
            xcopies[stream, d, o] = remote(
                xs.at[stream, part],
                xr.at[stream, part],
                x_ss.at[stream, d, o],
                x_rs.at[stream, d, o],
                x_peer(o),
            )

    def ring_rows(stream, way, k):
        return zbuf[stream, way, offs[k - 1] : offs[k], :]

    def arrive(stream, k):
        for way in range(2):
            hops[stream, way, k].wait_recv()
        if k < 4:
            hop(stream, k + 1)
            gather(stream, k, [(ring_rows(stream, 0, k), 0)])
            gather(stream, NZ - k, [(ring_rows(stream, 1, k), 0)])
        else:
            gather(stream, 4, [(ring_rows(stream, 0, 4), 0), (ring_rows(stream, 1, 4), 128)])

    def slots_ready(stream, half):
        for d in ORDER[4 * half : 4 * half + 4]:
            for o in range(1, NX):
                xcopies[stream, d, o].wait_recv()

    HALF = 4 * CLS
    nt = lambda a, b: lax.dot_general(
        a, b, (((1,), (1,)), ((), ())), preferred_element_type=F32
    )
    nn = lambda a, b: jnp.dot(a, b, preferred_element_type=F32)
    ycopies = {}

    def keep(stream, src, half, cols, out):
        out = out.astype(BF16)
        xr[src, half * HALF : (half + 1) * HALF, cols] = out
        for p in range(4):
            base = half * HALF + p * CLS
            yr[stream, base : base + CAP, cols] = out[p * CLS : p * CLS + CAP]

    def send_back(stream, src, half):
        for d in reversed(ORDER[4 * half : 4 * half + 4]):
            base = ORDER.index(d) * CLS
            for o in range(1, NX):
                part = pl.ds(base + o * CAP, CAP)
                ycopies[stream, d, o] = remote(
                    xr.at[src, part],
                    yr.at[stream, part],
                    y_ss.at[stream, d, o],
                    y_rs.at[stream, d, o],
                    x_peer(-o),
                )

    def backward(half):
        rows = slice(half * HALF, (half + 1) * HALF)

        @pl.loop(0, HID // 256)
        def _(b):
            cols = pl.ds(pl.multiple_of(b * 256, 256), 256)
            gate_act = nn(xr[R_, rows, :], wg[:, cols])
            up_act = nn(xr[R_, rows, :], wu[:, cols])
            hid_grad = nt(xr[C_, rows, :], wd[cols, :])
            sigma = jax.nn.sigmoid(gate_act)
            hid[0, :, cols] = (
                hid_grad * up_act * sigma * (1.0 + gate_act * (1.0 - sigma))
            ).astype(BF16)
            hid[1, :, cols] = (hid_grad * gate_act * sigma).astype(BF16)

        @pl.loop(0, D // 256)
        def _(b):
            cols = pl.ds(pl.multiple_of(b * 256, 256), 256)
            keep(G_, R_, half, cols, nt(hid[0], wg[cols, :]) + nt(hid[1], wu[cols, :]))

        send_back(G_, R_, half)

    def forward(half):
        rows = slice(half * HALF, (half + 1) * HALF)

        @pl.loop(0, HID // 256)
        def _(b):
            cols = pl.ds(pl.multiple_of(b * 256, 256), 256)
            gate_act = nn(xr[F_, rows, :], wg[:, cols])
            up_act = nn(xr[F_, rows, :], wu[:, cols])
            hid[0, :, cols] = (jax.nn.silu(gate_act) * up_act).astype(BF16)

        @pl.loop(0, D // 256)
        def _(b):
            cols = pl.ds(pl.multiple_of(b * 256, 256), 256)
            keep(O_, F_, half, cols, nn(hid[0], wd[:, cols]))

        send_back(O_, F_, half)

    def class_rows(stream, d, n, base):
        for o in range(1, NX):
            if (stream, d, o) in ycopies:
                ycopies.pop((stream, d, o)).wait_recv()
        m = 0 if stream == O_ else 1
        start = ORDER.index(d) * CLS
        values = yr[stream, start : start + CLS, :]
        if stream == O_:
            values = (values.astype(F32) * meta_t[0:CLS, 8 * d + 1 : 8 * d + 2]).astype(BF16)
        index = meta[8 * d + 2 * m : 8 * d + 2 * m + 1, 0:CLS]
        sel = one(index == (iota((n, CLS), 0) + base).astype(F32)).astype(BF16)
        return jnp.dot(sel, values, preferred_element_type=F32)

    backs = {}

    def combine(stream, k):
        for way in range(2):
            n = caps[k - 1]
            d = k if way == 0 else NZ - k
            total = class_rows(stream, d, n, 128 * way if k == 4 else 0)
            part = slice(offs[k - 1], offs[k])
            if k < 4:
                backs[stream, way, k + 1].wait_recv()
                more = caps[k]
                near = rb[stream, way, offs[k] : offs[k + 1], :].astype(F32)
                head = (total[:more] + near).astype(BF16)
                sb[stream, way, offs[k - 1] : offs[k - 1] + more, :] = head
                if more < n:
                    sb[stream, way, offs[k - 1] + more : offs[k], :] = total[more:].astype(BF16)
            else:
                sb[stream, way, part, :] = total.astype(BF16)
            part = pl.ds(offs[k - 1], n)
            backs[stream, way, k] = remote(
                sb.at[stream, way, part],
                rb.at[stream, way, part],
                r_ss.at[stream, way, k - 1],
                r_rs.at[stream, way, k - 1],
                z_peer(2 * way - 1),
            )

    def home(stream):
        m = 0 if stream == O_ else 1
        total = class_rows(stream, 0, TOK, 0)
        for way in range(2):
            backs[stream, way, 1].wait_recv()
            col = pos_t[:, 2 * m + way : 2 * m + way + 1]
            sel = one(col == iota((TOK, caps[0]), 1).astype(F32)).astype(BF16)
            total = total + jnp.dot(
                sel, rb[stream, way, 0 : caps[0], :], preferred_element_type=F32
            )
        return total

    rows, scale = normalize(saved)
    scale_ref[...] = scale
    sort_rows(R_, rows)
    hop(R_, 1)
    gather(R_, 0, [(rows, 0)])
    sort_rows(C_, upstream[...])
    hop(C_, 1)
    gather(C_, 0, [(upstream[...], 0)])
    rows, unused = normalize(arriving)
    sort_rows(F_, rows)
    gather(F_, 0, [(rows, 0)])
    arrive(R_, 1)
    arrive(C_, 1)
    hop(F_, 1)
    arrive(R_, 2)
    arrive(C_, 2)
    arrive(F_, 1)
    arrive(R_, 3)
    arrive(C_, 3)
    arrive(F_, 2)
    arrive(R_, 4)
    arrive(C_, 4)
    for copy in weights:
        copy.wait()
    slots_ready(R_, 0)
    slots_ready(C_, 0)
    backward(0)
    arrive(F_, 3)
    slots_ready(R_, 1)
    slots_ready(C_, 1)
    backward(1)
    arrive(F_, 4)
    combine(G_, 4)
    slots_ready(F_, 0)
    forward(0)
    combine(G_, 3)
    slots_ready(F_, 1)
    forward(1)
    combine(G_, 2)
    combine(O_, 4)
    combine(G_, 1)
    combine(O_, 3)
    total = home(G_)
    gained = gain[...] * total
    values = saved[...].astype(F32)
    scale = scale_ref[...]
    cube = scale * scale * scale
    grad[...] = (
        upstream[...].astype(F32)
        + scale * gained
        - values * cube * jnp.mean(values * gained, axis=1, keepdims=True)
    ).astype(BF16)
    combine(O_, 2)
    combine(O_, 1)
    act[...] = (arriving[...].astype(F32) + home(O_)).astype(BF16)
    for copy in sends:
        copy.wait_send()


def layer(caps, cid, *args):
    vmem = pl.BlockSpec(memory_space=pltpu.VMEM)
    hbm = pl.BlockSpec(memory_space=pl.ANY)
    rows = jax.ShapeDtypeStruct((TOK, D), BF16)
    sem = pltpu.SemaphoreType.DMA
    total = sum(caps)
    slots = NZ * CLS
    return pl.pallas_call(
        functools.partial(layer_kernel, caps),
        out_shape=(rows, rows),
        in_specs=[vmem] * 8 + [hbm] * 3,
        out_specs=(vmem, vmem),
        scratch_shapes=[
            pltpu.VMEM((D, HID), BF16),
            pltpu.VMEM((D, HID), BF16),
            pltpu.VMEM((HID, D), BF16),
            pltpu.VMEM((3, 2, TOK, D), BF16),
            pltpu.VMEM((3, 2, total, D), BF16),
            pltpu.VMEM((3, slots, D), BF16),
            pltpu.VMEM((3, slots, D), BF16),
            pltpu.VMEM((2, slots, D), BF16),
            pltpu.VMEM((2, 2, total, D), BF16),
            pltpu.VMEM((2, 2, total, D), BF16),
            pltpu.VMEM((2, 4 * CLS, HID), BF16),
            pltpu.VMEM((TOK, 1), F32),
            sem((3,)),
            sem((3, 2, 4)),
            sem((3, 2, 4)),
            sem((3, NZ, NX)),
            sem((3, NZ, NX)),
            sem((2, NZ, NX)),
            sem((2, NZ, NX)),
            sem((2, 2, 4)),
            sem((2, 2, 4)),
        ],
        name="layer%d" % cid,
        compiler_params=pltpu.CompilerParams(
            collective_id=cid, has_side_effects=True, vmem_limit_bytes=67043328
        ),
    )(*args)


def local(
    handoff,
    cotangent_handoff,
    saved_input,
    norm_gain,
    w_gate,
    w_up,
    w_down,
    picks_fwd,
    picks_bwd,
    gates_fwd,
    gates_bwd,
):
    caps = FULL
    arriving, upstream, meta, meta_t, pos, pos_t, flag = prepare(
        caps,
        handoff[0],
        cotangent_handoff[0],
        picks_fwd[0].T,
        gates_fwd[0].T,
        picks_bwd[0].T,
        gates_bwd[0].T,
    )
    args = (
        saved_input[0],
        arriving,
        upstream,
        norm_gain,
        meta,
        meta_t,
        pos,
        pos_t,
        w_gate[0, 0],
        w_up[0, 0],
        w_down[0, 0],
    )
    act, grad = layer(FULL, 1, *args)
    return (act[None], grad[None])


def solution(mesh):
    in_specs = (
        P("section", "expert", None),
        P("section", "expert", None),
        P("section", "expert", None),
        P("section", None),
        P("section", "expert", None, None),
        P("section", "expert", None, None),
        P("section", "expert", None, None),
        P("section", "expert", None),
        P("section", "expert", None),
        P("section", "expert", None),
        P("section", "expert", None),
    )
    out_specs = (P("section", "expert", None), P("section", "expert", None))
    return jax.shard_map(local, mesh=mesh, in_specs=in_specs, out_specs=out_specs, check_vma=False)
```

```python
import functools

import jax
import jax.numpy as jnp
from jax import lax
from jax.experimental import pallas as pl
from jax.experimental.pallas import tpu as pltpu
from jax.sharding import PartitionSpec as P

EPS = 1e-06
MESH = pl.DeviceIdType.MESH
F32 = jnp.float32
BF16 = jnp.bfloat16

NX = 4
NZ = 8
SEC = 8
CAP = 16
TOK = 128
D = 2048
HID = 768
CLS = 4 * CAP
CH = 2
DC = D // CH
FULL = (128, 128, 128, 64)
USUAL = (104, 88, 64, 40)
ORDER = (0, 1, 7, 2, 6, 3, 5, 4)


def where_am_i():
    e = lax.axis_index("expert")
    return lax.axis_index("section"), e // NZ, e % NZ


def at(s, x, z):
    return (s, x * NZ + z)


def iota(shape, dim):
    return lax.broadcasted_iota(jnp.int32, shape, dim)


def one(cond):
    return jnp.where(cond, jnp.float32(1.0), jnp.float32(0.0))


def routing(picks, gates, x, z):
    tok = iota((TOK, TOK), 1)
    sub = iota((TOK, TOK), 0)
    weight = gates / jnp.sum(gates, axis=0, keepdims=True)
    lane_e = iota((32, TOK), 0)
    disp = lane_e // 4
    expert = ((x + lane_e % 4) % NX) * NZ + (z + disp) % NZ
    named = jnp.zeros((32, TOK), F32)
    share = jnp.zeros((32, TOK), F32)
    for j in range(picks.shape[0]):
        hit = picks[j : j + 1, :] == expert
        named = named + one(hit)
        share = share + jnp.where(hit, weight[j : j + 1, :], 0.0)
    place = jnp.dot(
        named.astype(BF16), one(sub < tok).astype(BF16), preferred_element_type=F32
    )
    dist = disp.astype(F32)
    up = jnp.max(named * jnp.where(disp < 4, dist, 0.0), axis=0, keepdims=True)
    down = jnp.max(named * jnp.where(disp > 4, 8.0 - dist, 0.0), axis=0, keepdims=True)
    far = jnp.max(jnp.where(disp == 4, named, 0.0), axis=0, keepdims=True)
    lighter = jnp.sum(up, axis=1, keepdims=True) < jnp.sum(down, axis=1, keepdims=True)
    lighter = jnp.broadcast_to(one(lighter), (1, TOK))
    go_up = jnp.where(up == down, lighter, one(up > down))
    up = jnp.where(far * go_up > 0.0, 4.0, up)
    down = jnp.where(far * (1.0 - go_up) > 0.0, 4.0, down)

    def ranks(reach):
        row = jnp.broadcast_to(reach, (TOK, TOK))
        col = jnp.sum(jnp.where(sub == tok, row, 0.0), axis=1, keepdims=True)
        col = jnp.broadcast_to(col, (TOK, TOK))
        ahead = jnp.where(row > col, 1.0, jnp.where(row == col, one(tok < sub), 0.0))
        pos_col = jnp.sum(ahead, axis=1, keepdims=True)
        ahead = jnp.where(col > row, 1.0, jnp.where(row == col, one(sub < tok), 0.0))
        pos_row = jnp.sum(ahead, axis=0, keepdims=True)
        return pos_row, pos_col

    up_row, up_col = ranks(up)
    down_row, down_col = ranks(down)
    own = iota((1, TOK), 1).astype(F32)
    split = jnp.where(go_up > 0.0, up_row, down_row + 128.0)
    value = jnp.where(
        disp == 0, own, jnp.where(disp < 4, up_row, jnp.where(disp == 4, split, down_row))
    )
    slot = iota((32, CAP, TOK), 1).astype(F32)
    chosen = jnp.where(place[:, None, :] == slot, named[:, None, :], 0.0)
    index = jnp.sum(chosen * (value + 1.0)[:, None, :], axis=2, keepdims=True) - 1.0
    scale = jnp.sum(chosen * share[:, None, :], axis=2, keepdims=True)
    index = index.reshape(32 * CAP, 1)
    scale = scale.reshape(32 * CAP, 1)
    return index, scale, (up_row, down_row), (up_col, down_col), (up, down)


def remote_copies():
    sends = []

    def remote(src, dst, send, recv, peer):
        copy = pltpu.make_async_remote_copy(
            src, dst, send, recv, device_id=peer, device_id_type=MESH
        )
        copy.start()
        sends.append(copy)
        return copy

    return remote, sends


def normalized(ref, gain):
    values = ref[...].astype(F32)
    scale = lax.rsqrt(jnp.mean(values * values, axis=-1, keepdims=True) + EPS)
    return (values * scale * gain[...]).astype(BF16), scale


class Dispatch:
    def __init__(self, caps, m, remote, first, zbuf, xs, xr, z_ss, z_rs, x_ss, x_rs, meta_t, scaled):
        self.caps, self.m, self.remote = caps, m, remote
        self.first, self.zbuf, self.xs, self.xr = first, zbuf, xs, xr
        self.z_ss, self.z_rs, self.x_ss, self.x_rs = z_ss, z_rs, x_ss, x_rs
        self.meta_t, self.scaled = meta_t, scaled
        self.offs = [sum(caps[:k]) for k in range(5)]
        self.s, self.x, self.z = where_am_i()
        self.hops, self.xcopies = {}, {}

    def sort(self, rows, pos):
        for way in range(2):
            order = pos[2 * self.m + way : 2 * self.m + way + 1, :]
            perm = one(order == iota((TOK, TOK), 0).astype(F32)).astype(BF16)
            for c in range(CH):
                part = rows[:, c * DC : (c + 1) * DC]
                self.first[way, c] = jnp.dot(perm, part, preferred_element_type=F32).astype(BF16)

    def hop(self, k, c):
        caps, offs = self.caps, self.offs
        for way in range(2):
            if k == 1:
                src = self.first.at[way, c, pl.ds(0, caps[0])]
            else:
                src = self.zbuf.at[way, c, pl.ds(offs[k - 2], caps[k - 1])]
            self.hops[way, k, c] = self.remote(
                src,
                self.zbuf.at[way, c, pl.ds(offs[k - 1], caps[k - 1])],
                self.z_ss.at[way, k - 1, c],
                self.z_rs.at[way, k - 1, c],
                at(self.s, self.x, (self.z + 1 - 2 * way + NZ) % NZ),
            )

    def gather(self, d, c, rows):
        col = 8 * d + 2 * self.m
        index = self.meta_t[0:CLS, col : col + 1]
        total = None
        for values, base in rows:
            n = values.shape[0]
            sel = one(index == (iota((CLS, n), 1) + base).astype(F32)).astype(BF16)
            part = jnp.dot(sel, values, preferred_element_type=F32)
            total = part if total is None else total + part
        if self.scaled:
            total = total * self.meta_t[0:CLS, col + 1 : col + 2]
        total = total.astype(BF16)
        base = ORDER.index(d) * CLS
        cols = slice(c * DC, (c + 1) * DC)
        self.xr[base : base + CAP, cols] = total[0:CAP]
        self.xs[c, base + CAP : base + CLS, :] = total[CAP:CLS]
        for o in range(1, NX):
            part = pl.ds(base + o * CAP, CAP)
            self.xcopies[d, o, c] = self.remote(
                self.xs.at[c, part],
                self.xr.at[part, pl.ds(c * DC, DC)],
                self.x_ss.at[d, o, c],
                self.x_rs.at[d, o, c],
                at(self.s, (self.x + o) % NX, self.z),
            )

    def ring_rows(self, way, k, c):
        return self.zbuf[way, c, self.offs[k - 1] : self.offs[k], :]

    def arrive(self, k, c):
        for way in range(2):
            self.hops[way, k, c].wait_recv()
        if k < 4:
            self.hop(k + 1, c)
            self.gather(k, c, [(self.ring_rows(0, k, c), 0)])
            self.gather(NZ - k, c, [(self.ring_rows(1, k, c), 0)])
        else:
            self.gather(4, c, [(self.ring_rows(0, 4, c), 0), (self.ring_rows(1, 4, c), 128)])

    def own(self, rows):
        for c in range(CH):
            self.gather(0, c, [(rows[:, c * DC : (c + 1) * DC], 0)])

    def slots_ready(self, half):
        for d in ORDER[4 * half : 4 * half + 4]:
            for o in range(1, NX):
                for c in range(CH):
                    self.xcopies[d, o, c].wait_recv()


def dispatch_scratch(caps, streams):
    sem = pltpu.SemaphoreType.DMA
    return [
        pltpu.VMEM((streams, 2, CH, TOK, DC), BF16),
        pltpu.VMEM((streams, 2, CH, sum(caps), DC), BF16),
        pltpu.VMEM((streams, CH, NZ * CLS, DC), BF16),
        sem((streams, 2, 4, CH)),
        sem((streams, 2, 4, CH)),
        sem((streams, NZ, NX, CH)),
        sem((streams, NZ, NX, CH)),
    ]


def prepare_kernel(
    caps,
    handoff,
    cotangent,
    saved,
    gain,
    picks_f,
    gates_f,
    picks_b,
    gates_b,
    arriving,
    upstream,
    xr,
    meta,
    meta_t,
    pos,
    pos_t,
    flag,
    first,
    zbuf,
    xs,
    z_ss,
    z_rs,
    xd_ss,
    xd_rs,
    meta_send,
    flag_x,
    flag_s,
    big_send,
    big_recv,
    meta_ss,
    meta_rs,
    x_ss,
    x_rs,
    s_ss,
    s_rs,
):
    s, x, z = where_am_i()
    z_peer = lambda d: at(s, x, (z + d) % NZ)
    x_peer = lambda d: at(s, (x + d) % NX, z)
    s_peer = lambda d: at((s + d) % SEC, x, z)
    barrier = pltpu.get_barrier_semaphore()
    partners = (
        [z_peer(d) for d in range(1, NZ)]
        + [x_peer(d) for d in range(1, NX)]
        + [s_peer(d) for d in range(1, SEC)]
    )
    for peer in partners:
        pl.semaphore_signal(barrier, inc=1, device_id=peer, device_id_type=MESH)
    table, over = jnp.zeros((CLS, TOK), F32), jnp.zeros((1, 1), F32)
    lane, lane_t = iota((CLS, TOK), 1), iota((TOK, TOK), 1)
    columns = jnp.zeros((TOK, TOK), F32)
    pos[...] = jnp.zeros((8, TOK), F32)
    rows, unused = normalized(saved, gain)
    remote, sends = remote_copies()
    stream, cots = [
        Dispatch(
            caps, 1, remote, first.at[i], zbuf.at[i], xs.at[i], xr.at[i],
            z_ss.at[i], z_rs.at[i], xd_ss.at[i], xd_rs.at[i], meta_t, i == 1,
        )
        for i in range(2)
    ]
    for m, (picks, gates) in ((1, (picks_b, gates_b)), (0, (picks_f, gates_f))):
        index, scale, order, cols, reach = routing(picks[...], gates[...], x, z)
        for i in range(2):
            pos[2 * m + i : 2 * m + i + 1, :] = order[i]
            columns = jnp.where(lane_t == 2 * m + i, cols[i], columns)
            for k in range(4):
                count = jnp.sum(one(reach[i] > k + 0.5), axis=1, keepdims=True)
                over = jnp.maximum(over, one(count > caps[k] + 0.5))
        for d in range(NZ):
            part = slice(d * CLS, (d + 1) * CLS)
            table = jnp.where(lane == 8 * d + 2 * m, index[part], table)
            table = jnp.where(lane == 8 * d + 2 * m + 1, scale[part], table)
    pos_t[...] = columns
    whole = jnp.concatenate([table, jnp.zeros((CLS, TOK), F32)], axis=0)
    whole = jnp.transpose(whole)[:CLS, :]
    fifth = iota((CLS, TOK), 0) % 8 == 4
    whole = jnp.where(fifth, jnp.broadcast_to(over, (CLS, TOK)), whole)
    meta_send[...] = whole
    meta[0:8, :] = whole[0:8, :]
    copies = []
    pl.semaphore_wait(barrier, len(partners))
    for d in range(1, NZ):
        part = pl.ds(8 * d, 8)
        copies.append(
            remote(meta_send.at[part], meta.at[part], meta_ss.at[d], meta_rs.at[d], z_peer(d))
        )
    back = remote(cotangent, upstream, big_send.at[1], big_recv.at[1], s_peer(SEC - 1))
    stream.sort(rows, pos)
    for c in range(CH):
        stream.hop(1, c)
    for copy in copies:
        copy.wait_recv()
    got = meta[...]
    meta_t[...] = jnp.transpose(jnp.concatenate([got, jnp.zeros((CLS, TOK), F32)], axis=0))
    over = jnp.max(jnp.where(fifth, got, 0.0), axis=0, keepdims=True)

    def spread(over, buf, peers, send, recv):
        buf[0] = jnp.broadcast_to(over, (8, TOK))
        return [
            remote(buf.at[0], buf.at[d], send.at[d], recv.at[d], peer)
            for d, peer in enumerate(peers, 1)
        ]

    def collect(buf, copies):
        for copy in copies:
            copy.wait_recv()
        return jnp.max(jnp.max(buf[...], axis=0), axis=0, keepdims=True)

    copies = spread(over, flag_x, [x_peer(d) for d in range(1, NX)], x_ss, x_rs)
    stream.own(rows)
    stream.arrive(1, 0)
    over = collect(flag_x, copies)
    copies = spread(over, flag_s, [s_peer(d) for d in range(1, SEC)], s_ss, s_rs)
    ahead = remote(handoff, arriving, big_send.at[0], big_recv.at[0], s_peer(1))
    both = range(CH)
    for c in both[1:]:
        stream.arrive(1, c)
    back.wait_recv()
    cots.sort(upstream[...], pos)
    for c in both:
        cots.hop(1, c)
    cots.own(upstream[...])
    for which, k in (
        (stream, 2), (stream, 3), (cots, 1), (stream, 4), (cots, 2), (cots, 3), (cots, 4)
    ):
        for c in both:
            which.arrive(k, c)
    over = collect(flag_s, copies)
    flag[0, 0] = jnp.max(over)
    for half in range(2):
        stream.slots_ready(half)
        cots.slots_ready(half)
    ahead.wait_recv()
    for copy in sends:
        copy.wait_send()


def prepare(caps, *args):
    vmem = pl.BlockSpec(memory_space=pltpu.VMEM)
    smem = pl.BlockSpec(memory_space=pltpu.SMEM)
    hbm = pl.BlockSpec(memory_space=pl.ANY)
    rows = jax.ShapeDtypeStruct((TOK, D), BF16)
    sem = pltpu.SemaphoreType.DMA
    return pl.pallas_call(
        functools.partial(prepare_kernel, caps),
        out_shape=(
            rows,
            rows,
            jax.ShapeDtypeStruct((2, NZ * CLS, D), BF16),
            jax.ShapeDtypeStruct((CLS, TOK), F32),
            jax.ShapeDtypeStruct((TOK, TOK), F32),
            jax.ShapeDtypeStruct((8, TOK), F32),
            jax.ShapeDtypeStruct((TOK, TOK), F32),
            jax.ShapeDtypeStruct((1, 1), F32),
        ),
        in_specs=[hbm, hbm] + [vmem] * 6,
        out_specs=(hbm,) + (vmem,) * 6 + (smem,),
        scratch_shapes=dispatch_scratch(caps, 2)
        + [
            pltpu.VMEM((CLS, TOK), F32),
            pltpu.VMEM((NX, 8, TOK), F32),
            pltpu.VMEM((SEC, 8, TOK), F32),
            sem((2,)),
            sem((2,)),
            sem((NZ,)),
            sem((NZ,)),
            sem((NX,)),
            sem((NX,)),
            sem((SEC,)),
            sem((SEC,)),
        ],
        name="prepare",
        compiler_params=pltpu.CompilerParams(collective_id=0, has_side_effects=True),
    )(*args)


G_, O_ = 0, 1


def layer_kernel(
    caps,
    complete,
    saved,
    arriving,
    upstream,
    gain,
    meta,
    meta_t,
    pos,
    pos_t,
    b_slots,
    w_gate,
    w_up,
    w_down,
    act,
    grad,
    first,
    zbuf,
    xs,
    z_ss,
    z_rs,
    x_ss,
    x_rs,
    wg,
    wu,
    wd,
    xr,
    yr,
    sb,
    rb,
    hid,
    w_sem,
    y_ss,
    y_rs,
    r_ss,
    r_rs,
):
    s, x, z = where_am_i()
    z_peer = lambda d: at(s, x, (z + d + NZ) % NZ)
    x_peer = lambda d: at(s, (x + d + NX) % NX, z)
    offs = [sum(caps[:k]) for k in range(5)]
    loads = [(w_gate, wg), (w_up, wu), (w_down, wd)]
    if complete:
        loads = [(b_slots.at[i], xr.at[i]) for i in range(2)] + loads
    loads = [pltpu.make_async_copy(src, dst, w_sem.at[i]) for i, (src, dst) in enumerate(loads)]
    for copy in loads:
        copy.start()
    barrier = pltpu.get_barrier_semaphore()
    partners = [z_peer(1), z_peer(-1), x_peer(1), x_peer(2), x_peer(3)]
    for peer in partners:
        pl.semaphore_signal(barrier, inc=1, device_id=peer, device_id_type=MESH)
    remote, sends = remote_copies()

    def stream(i, n, m, scaled):
        return Dispatch(
            caps, m, remote, first.at[i], zbuf.at[i], xs.at[i], xr.at[n],
            z_ss.at[i], z_rs.at[i], x_ss.at[i], x_rs.at[i], meta_t, scaled,
        )

    fwds = stream(0, 2, 0, False)
    HALF = 4 * CLS
    nt = lambda a, b: lax.dot_general(
        a, b, (((1,), (1,)), ((), ())), preferred_element_type=F32
    )
    nn = lambda a, b: jnp.dot(a, b, preferred_element_type=F32)
    ycopies = {}

    def keep(which, src, half, cols, out):
        out = out.astype(BF16)
        xr[src, half * HALF : (half + 1) * HALF, cols] = out
        for p in range(4):
            base = half * HALF + p * CLS
            yr[which, base : base + CAP, cols] = out[p * CLS : p * CLS + CAP]

    def send_back(which, src, half):
        for d in reversed(ORDER[4 * half : 4 * half + 4]):
            base = ORDER.index(d) * CLS
            for o in range(1, NX):
                part = pl.ds(base + o * CAP, CAP)
                ycopies[which, d, o] = remote(
                    xr.at[src, part],
                    yr.at[which, part],
                    y_ss.at[which, d, o],
                    y_rs.at[which, d, o],
                    x_peer(-o),
                )

    def backward_hidden(half):
        rows = slice(half * HALF, (half + 1) * HALF)

        @pl.loop(0, HID // 256)
        def _(b):
            cols = pl.ds(pl.multiple_of(b * 256, 256), 256)
            gate_act = nn(xr[0, rows, :], wg[:, cols])
            up_act = nn(xr[0, rows, :], wu[:, cols])
            hid_grad = nt(xr[1, rows, :], wd[cols, :])
            sigma = jax.nn.sigmoid(gate_act)
            hid[0, :, cols] = (
                hid_grad * up_act * sigma * (1.0 + gate_act * (1.0 - sigma))
            ).astype(BF16)
            hid[1, :, cols] = (hid_grad * gate_act * sigma).astype(BF16)

    def backward_rows(half):
        @pl.loop(0, D // 256)
        def _(b):
            cols = pl.ds(pl.multiple_of(b * 256, 256), 256)
            keep(G_, 0, half, cols, nt(hid[0], wg[cols, :]) + nt(hid[1], wu[cols, :]))

    def forward_hidden(half):
        rows = slice(half * HALF, (half + 1) * HALF)

        @pl.loop(0, HID // 256)
        def _(b):
            cols = pl.ds(pl.multiple_of(b * 256, 256), 256)
            gate_act = nn(xr[2, rows, :], wg[:, cols])
            up_act = nn(xr[2, rows, :], wu[:, cols])
            hid[0, :, cols] = (jax.nn.silu(gate_act) * up_act).astype(BF16)

    def forward_rows(half):
        @pl.loop(0, D // 256)
        def _(b):
            cols = pl.ds(pl.multiple_of(b * 256, 256), 256)
            keep(O_, 2, half, cols, nn(hid[0], wd[:, cols]))

        send_back(O_, 2, half)

    def class_rows(which, d, c, n, base):
        for o in range(1, NX):
            if (which, d, o) in ycopies:
                ycopies.pop((which, d, o)).wait_recv()
        m = 0 if which == O_ else 1
        start = ORDER.index(d) * CLS
        values = yr[which, start : start + CLS, c * DC : (c + 1) * DC]
        if which == O_:
            values = (values.astype(F32) * meta_t[0:CLS, 8 * d + 1 : 8 * d + 2]).astype(BF16)
        index = meta[8 * d + 2 * m : 8 * d + 2 * m + 1, 0:CLS]
        sel = one(index == (iota((n, CLS), 0) + base).astype(F32)).astype(BF16)
        return jnp.dot(sel, values, preferred_element_type=F32)

    backs = {}

    def combine(which, k, c):
        for way in range(2):
            n = caps[k - 1]
            total = class_rows(which, k if way == 0 else NZ - k, c, n, 128 * way if k == 4 else 0)
            start = offs[k - 1]
            if k < 4:
                backs[which, way, k + 1, c].wait_recv()
                more = caps[k]
                near = rb[which, way, c, offs[k] : offs[k + 1], :].astype(F32)
                sb[which, way, c, start : start + more, :] = (total[:more] + near).astype(BF16)
                if more < n:
                    sb[which, way, c, start + more : offs[k], :] = total[more:].astype(BF16)
            else:
                sb[which, way, c, start : offs[k], :] = total.astype(BF16)
            part = pl.ds(start, n)
            backs[which, way, k, c] = remote(
                sb.at[which, way, c, part],
                rb.at[which, way, c, part],
                r_ss.at[which, way, k - 1, c],
                r_rs.at[which, way, k - 1, c],
                z_peer(2 * way - 1),
            )

    def home(which, c):
        m = 0 if which == O_ else 1
        total = class_rows(which, 0, c, TOK, 0)
        for way in range(2):
            backs[which, way, 1, c].wait_recv()
            col = pos_t[:, 2 * m + way : 2 * m + way + 1]
            sel = one(col == iota((TOK, caps[0]), 1).astype(F32)).astype(BF16)
            total = total + jnp.dot(
                sel, rb[which, way, c, 0 : caps[0], :], preferred_element_type=F32
            )
        return total

    both = range(CH)
    rows, unused = normalized(arriving, gain)
    fwds.sort(rows, pos)
    pl.semaphore_wait(barrier, len(partners))
    for c in both:
        fwds.hop(1, c)
    fwds.own(rows)
    if not complete:
        for i in range(2):
            other = stream(1 + i, i, 1, i == 1)
            rows = upstream[...] if i == 1 else normalized(saved, gain)[0]
            other.sort(rows, pos)
            for c in both:
                other.hop(1, c)
            other.own(rows)
            for k in range(1, 5):
                for c in both:
                    other.arrive(k, c)
            for half in range(2):
                other.slots_ready(half)
    for copy in loads:
        copy.wait()
    backward_hidden(1)
    fwds.arrive(1, 0)
    backward_rows(1)
    send_back(G_, 0, 1)
    fwds.arrive(1, 1)
    backward_hidden(0)
    fwds.arrive(2, 0)
    backward_rows(0)
    fwds.arrive(2, 1)
    fwds.arrive(3, 0)
    fwds.arrive(3, 1)
    combine(G_, 4, 0)
    combine(G_, 4, 1)
    fwds.arrive(4, 0)
    fwds.arrive(4, 1)
    send_back(G_, 0, 0)
    combine(G_, 3, 0)
    combine(G_, 3, 1)
    fwds.slots_ready(1)
    forward_hidden(1)
    forward_rows(1)
    combine(G_, 2, 0)
    combine(G_, 2, 1)
    fwds.slots_ready(0)
    forward_hidden(0)
    combine(G_, 1, 0)
    forward_rows(0)
    combine(O_, 4, 0)
    combine(G_, 1, 1)
    combine(O_, 4, 1)
    for c in both:
        combine(O_, 3, c)
    total = jnp.concatenate([home(G_, c) for c in both], axis=1)
    gained = gain[...] * total
    values = saved[...].astype(F32)
    scale = lax.rsqrt(jnp.mean(values * values, axis=-1, keepdims=True) + EPS)
    cube = scale * scale * scale
    grad[...] = (
        upstream[...].astype(F32)
        + scale * gained
        - values * cube * jnp.mean(values * gained, axis=1, keepdims=True)
    ).astype(BF16)
    for k in (2, 1):
        for c in both:
            combine(O_, k, c)
    for c in both:
        cols = slice(c * DC, (c + 1) * DC)
        act[:, cols] = (arriving[:, cols].astype(F32) + home(O_, c)).astype(BF16)
    for copy in sends:
        copy.wait_send()


def layer(caps, complete, cid, *args):
    vmem = pl.BlockSpec(memory_space=pltpu.VMEM)
    hbm = pl.BlockSpec(memory_space=pl.ANY)
    rows = jax.ShapeDtypeStruct((TOK, D), BF16)
    sem = pltpu.SemaphoreType.DMA
    total = sum(caps)
    slots = NZ * CLS
    return pl.pallas_call(
        functools.partial(layer_kernel, caps, complete),
        out_shape=(rows, rows),
        in_specs=[vmem] * 8 + [hbm] * 4,
        out_specs=(vmem, vmem),
        scratch_shapes=dispatch_scratch(caps, 1 if complete else 3)
        + [
            pltpu.VMEM((D, HID), BF16),
            pltpu.VMEM((D, HID), BF16),
            pltpu.VMEM((HID, D), BF16),
            pltpu.VMEM((3, slots, D), BF16),
            pltpu.VMEM((2, slots, D), BF16),
            pltpu.VMEM((2, 2, CH, total, DC), BF16),
            pltpu.VMEM((2, 2, CH, total, DC), BF16),
            pltpu.VMEM((2, 4 * CLS, HID), BF16),
            sem((5,)),
            sem((2, NZ, NX)),
            sem((2, NZ, NX)),
            sem((2, 2, 4, CH)),
            sem((2, 2, 4, CH)),
        ],
        name="layer%d" % cid,
        compiler_params=pltpu.CompilerParams(
            collective_id=cid, has_side_effects=True, vmem_limit_bytes=67043328
        ),
    )(*args)


def handed_out(act, grad):
    def kernel(a, b, c, d):
        c[...] = a[...]
        d[...] = b[...]

    vmem = pl.BlockSpec(memory_space=pltpu.VMEM)
    rows = jax.ShapeDtypeStruct((TOK, D), BF16)
    return pl.pallas_call(
        kernel, out_shape=(rows, rows), in_specs=[vmem] * 2, out_specs=(vmem, vmem), name="results"
    )(act, grad)


def local(
    handoff,
    cotangent_handoff,
    saved_input,
    norm_gain,
    w_gate,
    w_up,
    w_down,
    picks_fwd,
    picks_bwd,
    gates_fwd,
    gates_bwd,
):
    caps = USUAL
    arriving, upstream, b_slots, meta, meta_t, pos, pos_t, flag = prepare(
        caps,
        handoff[0],
        cotangent_handoff[0],
        saved_input[0],
        norm_gain,
        picks_fwd[0].T,
        gates_fwd[0].T,
        picks_bwd[0].T,
        gates_bwd[0].T,
    )
    args = (
        saved_input[0],
        arriving,
        upstream,
        norm_gain,
        meta,
        meta_t,
        pos,
        pos_t,
        b_slots,
        w_gate[0, 0],
        w_up[0, 0],
        w_down[0, 0],
    )
    act, grad = lax.cond(
        flag[0, 0] > 0.5,
        lambda *a: tuple(layer(FULL, False, 2, *a)),
        lambda *a: tuple(layer(caps, True, 1, *a)),
        *args,
    )
    act, grad = handed_out(act, grad)
    return (act[None], grad[None])


def solution(mesh):
    in_specs = (
        P("section", "expert", None),
        P("section", "expert", None),
        P("section", "expert", None),
        P("section", None),
        P("section", "expert", None, None),
        P("section", "expert", None, None),
        P("section", "expert", None, None),
        P("section", "expert", None),
        P("section", "expert", None),
        P("section", "expert", None),
        P("section", "expert", None),
    )
    out_specs = (P("section", "expert", None), P("section", "expert", None))
    return jax.shard_map(local, mesh=mesh, in_specs=in_specs, out_specs=out_specs, check_vma=False)
```
